256 devices in a mesh: level: 4 (over y), sub: 16 (over z, core), rhs: 4 (over x).
Axes of the slice: x: 4, y: 4, z: 8, core: 2. Of those that a mesh axis runs over, the one named last changes fastest.
Arguments:
- rhs: float32 [4, 256, 256, 256], P('level', 'sub', 'rhs'), may hold values from -6 to 6
- lower_inv: bfloat16 [4, 256, 256, 256], P('level', 'sub'), may hold values from -0.25 to 2.1
- lower_off: bfloat16 [4, 256, 256, 256], P('level', 'sub'), may hold values from -0.25 to 0.25
- upper_inv: bfloat16 [4, 256, 256, 256], P('level', 'sub'), may hold values from -0.25 to 2.1
- upper_off: bfloat16 [4, 256, 256, 256], P('level', 'sub'), may hold values from -0.25 to 0.25
- ancestor: bfloat16 [256, 256, 256], P('sub', 'rhs'), may hold values from -6 to 6
- parent: int32 [3, 256], replicated, may hold values from 0 to 255, as said below
Outputs:
- solution: float32 [4, 256, 256, 256], P('level', 'sub', 'rhs')
- update: float32 [4, 256, 256, 256], P('level', 'sub', 'rhs')
The draws below stay inside these ranges and needn't reach their ends.
Inputs may be any that keep to these rules, and one draw needn't show every extreme that they name: parent[t, c] names a supernode of sub index c // 16 or of sub index (c // 16) XOR 2 ** (t mod 4), where supernode s has sub index s // 16; a parent may have no children or several.
All inputs are finite; a program needn't handle non-finite values.
Results may differ from the reference program's by a relative error of at most 0.009.
Values may be sent and summed in bfloat16 or wider, within the bound.
A program may use at most 64 MiB of HBM per device.

```python
import jax
import jax.numpy as jnp
from jax import lax

W = 256
R = 256
SN_DEV = 16
TIERS = 4
NODES = 256
SUB_BITS = 4
N_SUB = 16


def triangle_draw(key, lower):
    key_off, key_diag = jax.random.split(key)
    shape = (TIERS, NODES, W, W)
    off_part = jnp.clip(jax.random.normal(key_off, shape, jnp.float32) * (0.6 / W ** 0.5), -0.25, 0.25)
    diag_part = jnp.exp(jax.random.uniform(key_diag, (TIERS, NODES, W, 1), jnp.float32, -0.7, 0.7))
    row_index = lax.broadcasted_iota(jnp.int32, (W, W), 0)
    col_index = lax.broadcasted_iota(jnp.int32, (W, W), 1)
    if lower:
        keep_off = row_index > col_index
    else:
        keep_off = row_index < col_index
    on_diag = row_index == col_index
    return jnp.where(keep_off, off_part, 0.0) + jnp.where(on_diag, diag_part, 0.0)


def draw_lower_inv(key, part):
    return triangle_draw(jax.random.fold_in(key, 11), False).astype(jnp.bfloat16)


def draw_upper_inv(key, part):
    return triangle_draw(jax.random.fold_in(key, 23), True).astype(jnp.bfloat16)


def draw_parent(key, part):
    key_slot, key_side, key_flip = jax.random.split(jax.random.fold_in(key, 37), 3)
    shape = (TIERS - 1, N_SUB, SN_DEV)
    parent_slot = jax.random.randint(key_slot, shape, 0, SN_DEV)
    side_pick = jax.random.randint(key_side, shape, 0, 2)
    flip_bit = jax.random.randint(key_flip, (TIERS - 1, N_SUB, 1), 0, 2)
    child_index = lax.broadcasted_iota(jnp.int32, shape, 2)
    tier_index = lax.broadcasted_iota(jnp.int32, shape, 0)
    sub_index = lax.broadcasted_iota(jnp.int32, shape, 1)
    role = jnp.bitwise_xor(child_index, flip_bit)
    forced = child_index <= 1
    parent_slot = jnp.where(forced & (role == 0), SN_DEV - 1, parent_slot)
    parent_slot = jnp.where(forced & (role == 1), 0, parent_slot)
    side_pick = jnp.where(forced, role, side_pick)
    bit_number = tier_index % SUB_BITS
    partner = jnp.bitwise_xor(sub_index, jnp.left_shift(jnp.ones(shape, jnp.int32), bit_number))
    target = jnp.where(side_pick == 1, partner, sub_index)
    return (target * SN_DEV + parent_slot).reshape(TIERS - 1, NODES).astype(jnp.int32)


def steps_of(key, extent, cuts, smallest, top_value):
    def one(axis_at, shards_of):
        steps = jax.random.uniform(jax.random.fold_in(jax.random.fold_in(key, 6), axis_at), (shards_of,), jnp.float32, smallest / len(cuts), top_value / len(cuts))
        return jnp.repeat(jnp.exp(steps), extent[axis_at] // shards_of).reshape((-1,) + (1,) * (len(extent) - axis_at - 1))

    level = one(*cuts[0])
    for cut in cuts[1:]:
        level = level * one(*cut)
    return level


def scatter_about(rng, extent, spread, limit, cuts=(), dtype=jnp.bfloat16):
    loudness = steps_of(rng, extent, cuts, -0.22, 0.18) if cuts else 1.0
    result = jax.random.normal(rng, extent, jnp.float32) * spread * loudness
    return jnp.minimum(jnp.maximum(result, -limit), limit).astype(dtype)


def setup_inputs(seed: int = 0) -> dict:
    streams_of = jax.random.split(jax.random.key(seed), 8)
    rhs = scatter_about(streams_of[0], (TIERS, NODES, R, W), 1.0, 6.0, ((0, 4), (1, 16), (2, 4)), jnp.float32)
    lower_inv = draw_lower_inv(jax.random.fold_in(streams_of[7], 71), 0)
    lower_off = scatter_about(streams_of[2], (TIERS, NODES, W, W), (2 * W) ** -0.5, 0.25, ((0, 4), (1, 16)))
    upper_inv = draw_upper_inv(jax.random.fold_in(streams_of[7], 71), 0)
    upper_off = scatter_about(streams_of[4], (TIERS, NODES, W, W), (2 * W) ** -0.5, 0.25, ((0, 4), (1, 16)))
    ancestor = scatter_about(streams_of[5], (NODES, R, W), 1.0, 6.0, ((0, 16), (1, 4)))
    parent = draw_parent(jax.random.fold_in(streams_of[7], 71), 0)
    return dict(rhs=rhs, lower_inv=lower_inv, lower_off=lower_off, upper_inv=upper_inv, upper_off=upper_off, ancestor=ancestor, parent=parent)


def tier_product(left, right):
    return jnp.einsum("srw,swv->srv", left.astype(jnp.float32), right.astype(jnp.float32))


def reference(rhs, lower_inv, lower_off, upper_inv, upper_off, ancestor, parent):
    tiers = rhs.shape[0]
    count = rhs.shape[1]
    forwards = []
    updates = []
    incoming = jnp.zeros(rhs.shape[1:], jnp.float32)
    for tier in range(tiers):
        residue = (rhs[tier] - incoming).astype(jnp.bfloat16)
        forward = tier_product(residue, lower_inv[tier]).astype(jnp.bfloat16)
        update = tier_product(forward, lower_off[tier])
        forwards.append(forward)
        updates.append(update)
        if tier + 1 < tiers:
            incoming = jax.ops.segment_sum(update, parent[tier], num_segments=count)
    solutions = [None] * tiers
    rounded = ancestor
    for tier in reversed(range(tiers)):
        if tier == tiers - 1:
            above_rows = ancestor
        else:
            above_rows = jnp.take(rounded, parent[tier], axis=0)
        reduced = (forwards[tier].astype(jnp.float32) - tier_product(above_rows, upper_off[tier])).astype(jnp.bfloat16)
        solution_part = tier_product(reduced, upper_inv[tier])
        solutions[tier] = solution_part
        rounded = solution_part.astype(jnp.bfloat16)
    return jnp.stack(solutions), jnp.stack(updates)
```

```python
import functools

import jax
import jax.numpy as jnp
from jax import lax
from jax.experimental import pallas as pl
from jax.experimental.pallas import tpu as pltpu
from jax.sharding import PartitionSpec as P

MESH = pl.DeviceIdType.MESH
CHUNK = 8
LAG = 4


def other(sub, mask):
    return sub + mask - 2 * mask * ((sub // mask) % 2)


def kernel(
    parent, rhs_in, linv_in, loff_in, uinv_in, uoff_in, anc_in,
    sol_out, upd_out,
    rhs, linv, loff, uinv, uoff, anc, sol, upd,
    sel, res, fwd, snd, inc, crecv, hbuf, back, above, stage,
    in_sem, out_sem, fs, fr, bs, br, cs, cr,
):
    count, rows, width = rhs.shape
    size = CHUNK
    chunks = rows // size
    level = lax.axis_index("level")
    sub = lax.axis_index("sub")
    col = lax.axis_index("rhs")
    top = 3

    def at(lv, s):
        return (lv, s, col)

    def cut(k):
        return pl.ds(pl.multiple_of(k * size, size), size)

    loads = [
        pltpu.make_async_copy(rhs_in, rhs, in_sem.at[0]),
        pltpu.make_async_copy(linv_in, linv, in_sem.at[1]),
        pltpu.make_async_copy(loff_in, loff, in_sem.at[2]),
        pltpu.make_async_copy(uoff_in, uoff, in_sem.at[3]),
        pltpu.make_async_copy(uinv_in, uinv, in_sem.at[4]),
    ]
    for load in loads[:3]:
        load.start()

    def anc_load(k):
        return pltpu.make_async_copy(
            anc_in.at[:, cut(k), :], anc.at[k], in_sem.at[5 + k]
        )

    barrier = pltpu.get_barrier_semaphore()
    friends = {
        0: [(0, 1), (1, 0)],
        1: [(0, 0), (2, 0), (2, 2)],
        2: [(1, 0), (1, 2), (3, 0), (3, 4)],
        3: [(2, 0), (2, 4)],
    }
    for lv, group in friends.items():
        @pl.when(level == lv)
        def _():
            for to, mask in group:
                there = other(sub, mask) if mask else sub
                pl.semaphore_signal(
                    barrier, inc=1, device_id=at(to, there), device_id_type=MESH
                )

    row = jnp.minimum(level, top - 1)
    codes = []
    for c in range(count):
        p = parent[row, sub * count + c]
        codes.append((p % count) + jnp.where(p // count == sub, 0, count))
    lane = lax.broadcasted_iota(jnp.int32, (1, count * size), 1)
    target = jnp.zeros((1, count * size), jnp.int32)
    for c in range(count):
        target = jnp.where(lane // size == c, codes[c], target)
    target = target * size + lane % size
    down = lax.broadcasted_iota(jnp.int32, (2 * count * size, count * size), 0)
    sel[...] = (down == target).astype(jnp.bfloat16)

    for lv, group in friends.items():
        @pl.when(level == lv)
        def _():
            pl.semaphore_wait(barrier, len(group))

    def remote(src, dst, ss, rs, to):
        return pltpu.make_async_remote_copy(
            src_ref=src, dst_ref=dst, send_sem=ss, recv_sem=rs,
            device_id=to, device_id_type=MESH,
        )

    def up_home(k, lv):
        return remote(
            snd.at[k, pl.ds(0, count)], inc.at[k, pl.ds(0, count)],
            fs.at[k, 0], fr.at[k, 0], at(lv + 1, sub),
        )

    def up_far(k, lv):
        return remote(
            snd.at[k, pl.ds(count, count)], inc.at[k, pl.ds(count, count)],
            fs.at[k, 1], fr.at[k, 1], at(lv + 1, other(sub, 2**lv)),
        )

    def down_home(k, lv):
        return remote(
            back.at[k], above.at[k, pl.ds(0, count)],
            bs.at[k, 0], br.at[k, 0], at(lv - 1, sub),
        )

    def down_far(k, lv):
        return remote(
            back.at[k], above.at[k, pl.ds(count, count)],
            bs.at[k, 1], br.at[k, 1], at(lv - 1, other(sub, 2 ** (lv - 1))),
        )

    def side_up(k):
        return remote(
            snd.at[k, pl.ds(count, count)], crecv.at[k],
            cs.at[k, 0], cr.at[k, 0], at(0, other(sub, 1)),
        )

    def side_down(k):
        return remote(
            above.at[k, pl.ds(0, count)], above.at[k, pl.ds(count, count)],
            cs.at[k, 1], cr.at[k, 1], at(0, other(sub, 1)),
        )

    def upd_store(k):
        return pltpu.make_async_copy(
            upd.at[:, cut(k), :], upd_out.at[:, cut(k), :], out_sem.at[k, 0]
        )

    def sol_store(k):
        return pltpu.make_async_copy(
            sol.at[:, cut(k), :], sol_out.at[:, cut(k), :], out_sem.at[k, 1]
        )

    def forward(k):
        @pl.when(k == 0)
        def _():
            loads[0].wait()

        @pl.when(level == 0)
        def _():
            res[...] = rhs[:, cut(k), :].astype(jnp.bfloat16)

        @pl.when(level == 1)
        def _():
            up_home(k, 0).wait_recv()
            got = inc[k, pl.ds(0, count)].astype(jnp.float32)
            res[...] = (rhs[:, cut(k), :] - got).astype(jnp.bfloat16)

        @pl.when(level >= 2)
        def _():
            up_home(k, 1).wait_recv()
            up_far(k, 1).wait_recv()
            got = inc[k, pl.ds(0, count)].astype(jnp.float32)
            got = got + inc[k, pl.ds(count, count)].astype(jnp.float32)
            res[...] = (rhs[:, cut(k), :] - got).astype(jnp.bfloat16)

        @pl.when(k == 0)
        def _():
            loads[1].wait()

        for c in range(count):
            part = jnp.dot(res[c], linv[c], preferred_element_type=jnp.float32)
            fwd[k, c] = part.astype(jnp.bfloat16)

        @pl.when(k == 0)
        def _():
            loads[2].wait()
            for load in loads[3:]:
                load.start()

        @pl.when((k == 0) & (level == top))
        def _():
            for j in range(chunks):
                anc_load(j).start()

        for c in range(count):
            upd[c, cut(k), :] = jnp.dot(
                fwd[k, c], loff[c], preferred_element_type=jnp.float32
            )
        upd_store(k).start()

        @pl.when(level < top)
        def _():
            moved = upd[:, cut(k), :].reshape(count * size, width)
            both = jnp.dot(
                sel[...], moved.astype(jnp.bfloat16), preferred_element_type=jnp.float32
            ).reshape(2 * count, size, width)
            snd[k] = both.astype(jnp.bfloat16)
            hbuf[k] = both[:count]

        @pl.when(level == 0)
        def _():
            side_up(k).start()

        for lv in (1, 2):
            @pl.when(level == lv)
            def _():
                up_far(k, lv).start()
                up_home(k, lv).start()

    def settle(k):
        side_up(k).wait_recv()
        total = hbuf[k] + crecv[k].astype(jnp.float32)
        snd[k, pl.ds(0, count)] = total.astype(jnp.bfloat16)
        up_home(k, 0).start()

    def backward(k):
        @pl.when(k == 0)
        def _():
            for load in loads[3:]:
                load.wait()

        @pl.when(level == top)
        def _():
            anc_load(k).wait()
            stage[pl.ds(0, count)] = anc[k]

        @pl.when((level == 1) | (level == 2))
        def _():
            down_home(k, 2).wait_recv()
            down_far(k, 2).wait_recv()
            stage[...] = above[k]

        @pl.when(level == 0)
        def _():
            down_home(k, 1).wait_recv()
            side_down(k).start()
            side_down(k).wait_recv()
            stage[...] = above[k]

        for c in range(count):
            where = jnp.where(level == top, c, codes[c])
            term = jnp.dot(stage[where], uoff[c], preferred_element_type=jnp.float32)
            res[c] = (fwd[k, c].astype(jnp.float32) - term).astype(jnp.bfloat16)
        for c in range(count):
            part = jnp.dot(res[c], uinv[c], preferred_element_type=jnp.float32)
            sol[c, cut(k), :] = part
            back[k, c] = part.astype(jnp.bfloat16)
        for lv in (1, 2, 3):
            @pl.when(level == lv)
            def _():
                if lv > 1:
                    down_far(k, lv).start()
                down_home(k, lv).start()
        sol_store(k).start()

    lag = jnp.where(level == top, 0, jnp.where(level == 2, min(LAG, chunks), chunks))

    def step(i, carry):
        @pl.when(i < chunks)
        def _():
            forward(i)

        @pl.when((level == 0) & (i >= 1) & (i <= chunks))
        def _():
            settle(i - 1)

        @pl.when(i >= lag)
        def _():
            backward(i - lag)

        return carry

    lax.fori_loop(0, chunks + lag, step, 0)

    def finish(k, carry):
        upd_store(k).wait()
        sol_store(k).wait()

        @pl.when(level == 0)
        def _():
            side_up(k).wait_send()
            side_down(k).wait_send()

        for lv in (0, 1, 2):
            @pl.when(level == lv)
            def _():
                up_home(k, lv).wait_send()
                if lv > 0:
                    up_far(k, lv).wait_send()

        for lv in (1, 2, 3):
            @pl.when(level == lv)
            def _():
                down_home(k, lv).wait_send()
                if lv > 1:
                    down_far(k, lv).wait_send()

        return carry

    lax.fori_loop(0, chunks, finish, 0)


def body(rhs, lower_inv, lower_off, upper_inv, upper_off, ancestor, parent):
    count, rows, width = rhs.shape[1:]
    size = CHUNK
    chunks = rows // size
    f32, b16 = jnp.float32, jnp.bfloat16
    block = jax.ShapeDtypeStruct((count, rows, width), f32)
    vm = pltpu.VMEM
    sem = pltpu.SemaphoreType.DMA
    anyspace = pl.BlockSpec(memory_space=pl.ANY)
    sol, upd = pl.pallas_call(
        kernel,
        out_shape=(block, block),
        in_specs=[pl.BlockSpec(memory_space=pltpu.SMEM)] + [anyspace] * 6,
        out_specs=(anyspace, anyspace),
        scratch_shapes=[
            vm((count, rows, width), f32),
            vm((count, width, width), b16),
            vm((count, width, width), b16),
            vm((count, width, width), b16),
            vm((count, width, width), b16),
            vm((chunks, count, size, width), b16),
            vm((count, rows, width), f32),
            vm((count, rows, width), f32),
            vm((2 * count * size, count * size), b16),
            vm((count, size, width), b16),
            vm((chunks, count, size, width), b16),
            vm((chunks, 2 * count, size, width), b16),
            vm((chunks, 2 * count, size, width), b16),
            vm((chunks, count, size, width), b16),
            vm((chunks, count, size, width), f32),
            vm((chunks, count, size, width), b16),
            vm((chunks, 2 * count, size, width), b16),
            vm((2 * count, size, width), b16),
            sem((5 + chunks,)),
            sem((chunks, 2)),
            sem((chunks, 2)),
            sem((chunks, 2)),
            sem((chunks, 2)),
            sem((chunks, 2)),
            sem((chunks, 2)),
            sem((chunks, 2)),
        ],
        compiler_params=pltpu.CompilerParams(
            collective_id=0, has_side_effects=True, vmem_limit_bytes=40 * 2**20
        ),
        name="tree_solve",
    )(parent, rhs[0], lower_inv[0], lower_off[0], upper_inv[0], upper_off[0], ancestor)
    return (sol[None], upd[None])


def solution(mesh):
    placed = (
        P("level", "sub", "rhs", None),
        P("level", "sub", None, None),
        P("level", "sub", None, None),
        P("level", "sub", None, None),
        P("level", "sub", None, None),
        P("sub", "rhs", None),
        P(),
    )
    return jax.shard_map(
        body,
        mesh=mesh,
        in_specs=placed,
        out_specs=(P("level", "sub", "rhs", None), P("level", "sub", "rhs", None)),
        check_vma=False,
    )
```

```python
import functools

import jax
import jax.numpy as jnp
from jax import lax
from jax.experimental import pallas as pl
from jax.experimental.pallas import tpu as pltpu
from jax.sharding import PartitionSpec as P

MESH = pl.DeviceIdType.MESH
CHUNK = 8
LAG = 4
UP_SIDE = ('all', 'all', 'all')
DOWN_SIDE = ('all', 'none', 'none')


def chosen(rule, k):
    if rule in ("all", "none"):
        return rule == "all"
    return k % 2 == (1 if rule == "odd" else 0)


def gate(condition, yes, no=None):
    if condition is True or condition is False:
        pick = yes if condition else no
        if pick is not None:
            pick()
        return
    pl.when(condition)(yes)
    if no is not None:
        pl.when(jnp.logical_not(condition))(no)


def other(sub, mask):
    return sub + mask - 2 * mask * ((sub // mask) % 2)


def kernel(
    parent, rhs_in, linv_in, loff_in, uinv_in, uoff_in, anc_in,
    sol_out, upd_out,
    rhs, linv, loff, uinv, uoff, anc, sol, upd,
    sel, res, fwd, snd, inc, crecv, hbuf, back, above, stage,
    in_sem, out_sem, fs, fr, bs, br, cs, cr,
):
    count, rows, width = rhs.shape
    size = CHUNK
    chunks = rows // size
    level = lax.axis_index("level")
    sub = lax.axis_index("sub")
    col = lax.axis_index("rhs")
    top = 3

    def at(lv, s):
        return (lv, s, col)

    def cut(k):
        return pl.ds(pl.multiple_of(k * size, size), size)

    loads = [
        pltpu.make_async_copy(rhs_in, rhs, in_sem.at[0]),
        pltpu.make_async_copy(linv_in, linv, in_sem.at[1]),
        pltpu.make_async_copy(loff_in, loff, in_sem.at[2]),
        pltpu.make_async_copy(uoff_in, uoff, in_sem.at[3]),
        pltpu.make_async_copy(uinv_in, uinv, in_sem.at[4]),
    ]
    for load in loads[:3]:
        load.start()

    def anc_load(k):
        return pltpu.make_async_copy(
            anc_in.at[:, cut(k), :], anc.at[k], in_sem.at[5 + k]
        )

    barrier = pltpu.get_barrier_semaphore()
    friends = {
        0: [(0, 1), (1, 0)],
        1: [(0, 0), (1, 2), (2, 0), (2, 2)],
        2: [(1, 0), (1, 2), (2, 4), (3, 0), (3, 4)],
        3: [(2, 0), (2, 4)],
    }
    for lv, group in friends.items():
        @pl.when(level == lv)
        def _():
            for to, mask in group:
                there = other(sub, mask) if mask else sub
                pl.semaphore_signal(
                    barrier, inc=1, device_id=at(to, there), device_id_type=MESH
                )

    row = jnp.minimum(level, top - 1)
    codes = []
    for c in range(count):
        p = parent[row, sub * count + c]
        codes.append((p % count) + jnp.where(p // count == sub, 0, count))
    lane = lax.broadcasted_iota(jnp.int32, (1, count * size), 1)
    target = jnp.zeros((1, count * size), jnp.int32)
    for c in range(count):
        target = jnp.where(lane // size == c, codes[c], target)
    target = target * size + lane % size
    down = lax.broadcasted_iota(jnp.int32, (2 * count * size, count * size), 0)
    sel[...] = (down == target).astype(jnp.bfloat16)

    for lv, group in friends.items():
        @pl.when(level == lv)
        def _():
            pl.semaphore_wait(barrier, len(group))

    def remote(src, dst, ss, rs, to):
        return pltpu.make_async_remote_copy(
            src_ref=src, dst_ref=dst, send_sem=ss, recv_sem=rs,
            device_id=to, device_id_type=MESH,
        )

    def up_home(k, lv):
        return remote(
            snd.at[k, pl.ds(0, count)], inc.at[k, pl.ds(0, count)],
            fs.at[k, 0], fr.at[k, 0], at(lv + 1, sub),
        )

    def up_far(k, lv):
        return remote(
            snd.at[k, pl.ds(count, count)], inc.at[k, pl.ds(count, count)],
            fs.at[k, 1], fr.at[k, 1], at(lv + 1, other(sub, 2**lv)),
        )

    def down_home(k, lv):
        return remote(
            back.at[k], above.at[k, pl.ds(0, count)],
            bs.at[k, 0], br.at[k, 0], at(lv - 1, sub),
        )

    def down_far(k, lv):
        return remote(
            back.at[k], above.at[k, pl.ds(count, count)],
            bs.at[k, 1], br.at[k, 1], at(lv - 1, other(sub, 2 ** (lv - 1))),
        )

    def side_up(k, lv):
        return remote(
            snd.at[k, pl.ds(count, count)], crecv.at[k],
            cs.at[k, 0], cr.at[k, 0], at(lv, other(sub, 2**lv)),
        )

    def side_down(k, lv):
        return remote(
            above.at[k, pl.ds(0, count)], above.at[k, pl.ds(count, count)],
            cs.at[k, 1], cr.at[k, 1], at(lv, other(sub, 2**lv)),
        )

    def upd_store(k):
        return pltpu.make_async_copy(
            upd.at[:, cut(k), :], upd_out.at[:, cut(k), :], out_sem.at[k, 0]
        )

    def sol_store(k):
        return pltpu.make_async_copy(
            sol.at[:, cut(k), :], sol_out.at[:, cut(k), :], out_sem.at[k, 1]
        )

    def forward(k):
        @pl.when(k == 0)
        def _():
            loads[0].wait()

        @pl.when(level == 0)
        def _():
            res[...] = rhs[:, cut(k), :].astype(jnp.bfloat16)

        @pl.when(level == 1)
        def _():
            up_home(k, 0).wait_recv()
            got = inc[k, pl.ds(0, count)].astype(jnp.float32)
            res[...] = (rhs[:, cut(k), :] - got).astype(jnp.bfloat16)

        for lv in (2, 3):
            @pl.when(level == lv)
            def _():
                up_home(k, lv - 1).wait_recv()
                got = inc[k, pl.ds(0, count)].astype(jnp.float32)

                def both():
                    up_far(k, lv - 1).wait_recv()
                    more = got + inc[k, pl.ds(count, count)].astype(jnp.float32)
                    res[...] = (rhs[:, cut(k), :] - more).astype(jnp.bfloat16)

                def single():
                    res[...] = (rhs[:, cut(k), :] - got).astype(jnp.bfloat16)

                gate(chosen(UP_SIDE[lv - 1], k), single, both)

        @pl.when(k == 0)
        def _():
            loads[1].wait()

        for c in range(count):
            part = jnp.dot(res[c], linv[c], preferred_element_type=jnp.float32)
            fwd[k, c] = part.astype(jnp.bfloat16)

        @pl.when(k == 0)
        def _():
            loads[2].wait()
            for load in loads[3:]:
                load.start()

        @pl.when((k == 0) & (level == top))
        def _():
            for j in range(chunks):
                anc_load(j).start()

        for c in range(count):
            upd[c, cut(k), :] = jnp.dot(
                fwd[k, c], loff[c], preferred_element_type=jnp.float32
            )
        upd_store(k).start()

        @pl.when(level < top)
        def _():
            moved = upd[:, cut(k), :].reshape(count * size, width)
            both = jnp.dot(
                sel[...], moved.astype(jnp.bfloat16), preferred_element_type=jnp.float32
            ).reshape(2 * count, size, width)
            snd[k] = both.astype(jnp.bfloat16)
            hbuf[k] = both[:count]

        for lv in (0, 1, 2):
            @pl.when(level == lv)
            def _():
                def straight():
                    up_far(k, lv).start()
                    up_home(k, lv).start()

                gate(
                    chosen(UP_SIDE[lv], k),
                    lambda: side_up(k, lv).start(), straight,
                )

    def settle(k, lv):
        side_up(k, lv).wait_recv()
        total = hbuf[k] + crecv[k].astype(jnp.float32)
        snd[k, pl.ds(0, count)] = total.astype(jnp.bfloat16)
        up_home(k, lv).start()

    def relay(k):
        for lv in (0, 1, 2):
            def go():
                down_home(k, lv + 1).wait_recv()
                side_down(k, lv).start()

            @pl.when(level == lv)
            def _():
                gate(chosen(DOWN_SIDE[lv], k), go)

    def backward(k):
        @pl.when(k == 0)
        def _():
            for load in loads[3:]:
                load.wait()

        @pl.when(level == top)
        def _():
            anc_load(k).wait()
            stage[pl.ds(0, count)] = anc[k]

        for lv in (0, 1, 2):
            def straight():
                down_home(k, lv + 1).wait_recv()
                down_far(k, lv + 1).wait_recv()

            @pl.when(level == lv)
            def _():
                gate(
                    chosen(DOWN_SIDE[lv], k),
                    lambda: side_down(k, lv).wait_recv(), straight,
                )
                stage[...] = above[k]

        for c in range(count):
            where = jnp.where(level == top, c, codes[c])
            term = jnp.dot(stage[where], uoff[c], preferred_element_type=jnp.float32)
            res[c] = (fwd[k, c].astype(jnp.float32) - term).astype(jnp.bfloat16)
        for c in range(count):
            part = jnp.dot(res[c], uinv[c], preferred_element_type=jnp.float32)
            sol[c, cut(k), :] = part
            back[k, c] = part.astype(jnp.bfloat16)
        for lv in (1, 2, 3):
            @pl.when(level == lv)
            def _():
                down_home(k, lv).start()
                gate(
                    chosen(DOWN_SIDE[lv - 1], k),
                    lambda: None, lambda: down_far(k, lv).start(),
                )
        sol_store(k).start()

    lag = jnp.where(level == top, -1, jnp.where(level == 2, min(LAG, chunks), chunks))

    def step(i, carry):
        @pl.when(i < chunks)
        def _():
            forward(i)

        for lv in (0, 1, 2):
            @pl.when((level == lv) & (i >= 1) & (i <= chunks))
            def _():
                gate(chosen(UP_SIDE[lv], i - 1), lambda: settle(i - 1, lv))

        @pl.when((i >= lag) & (i < chunks + lag))
        def _():
            relay(i - lag)

        @pl.when(i > lag)
        def _():
            backward(i - lag - 1)

        return carry

    lax.fori_loop(0, chunks + lag + 1, step, 0)

    def finish(k, carry):
        upd_store(k).wait()
        sol_store(k).wait()

        for lv in (0, 1, 2):
            @pl.when(level == lv)
            def _():
                up_home(k, lv).wait_send()
                gate(
                    chosen(UP_SIDE[lv], k),
                    lambda: side_up(k, lv).wait_send(),
                    lambda: up_far(k, lv).wait_send(),
                )
                gate(
                    chosen(DOWN_SIDE[lv], k),
                    lambda: side_down(k, lv).wait_send(),
                )

        for lv in (1, 2, 3):
            @pl.when(level == lv)
            def _():
                down_home(k, lv).wait_send()
                gate(
                    chosen(DOWN_SIDE[lv - 1], k),
                    lambda: None, lambda: down_far(k, lv).wait_send(),
                )

        return carry

    lax.fori_loop(0, chunks, finish, 0)


def body(rhs, lower_inv, lower_off, upper_inv, upper_off, ancestor, parent):
    count, rows, width = rhs.shape[1:]
    size = CHUNK
    chunks = rows // size
    f32, b16 = jnp.float32, jnp.bfloat16
    block = jax.ShapeDtypeStruct((count, rows, width), f32)
    vm = pltpu.VMEM
    sem = pltpu.SemaphoreType.DMA
    anyspace = pl.BlockSpec(memory_space=pl.ANY)
    sol, upd = pl.pallas_call(
        kernel,
        out_shape=(block, block),
        in_specs=[pl.BlockSpec(memory_space=pltpu.SMEM)] + [anyspace] * 6,
        out_specs=(anyspace, anyspace),
        scratch_shapes=[
            vm((count, rows, width), f32),
            vm((count, width, width), b16),
            vm((count, width, width), b16),
            vm((count, width, width), b16),
            vm((count, width, width), b16),
            vm((chunks, count, size, width), b16),
            vm((count, rows, width), f32),
            vm((count, rows, width), f32),
            vm((2 * count * size, count * size), b16),
            vm((count, size, width), b16),
            vm((chunks, count, size, width), b16),
            vm((chunks, 2 * count, size, width), b16),
            vm((chunks, 2 * count, size, width), b16),
            vm((chunks, count, size, width), b16),
            vm((chunks, count, size, width), f32),
            vm((chunks, count, size, width), b16),
            vm((chunks, 2 * count, size, width), b16),
            vm((2 * count, size, width), b16),
            sem((5 + chunks,)),
            sem((chunks, 2)),
            sem((chunks, 2)),
            sem((chunks, 2)),
            sem((chunks, 2)),
            sem((chunks, 2)),
            sem((chunks, 2)),
            sem((chunks, 2)),
        ],
        compiler_params=pltpu.CompilerParams(
            collective_id=0, has_side_effects=True, vmem_limit_bytes=62 * 2**20
        ),
        name="tree_solve",
    )(parent, rhs[0], lower_inv[0], lower_off[0], upper_inv[0], upper_off[0], ancestor)
    return (sol[None], upd[None])


def solution(mesh):
    placed = (
        P("level", "sub", "rhs", None),
        P("level", "sub", None, None),
        P("level", "sub", None, None),
        P("level", "sub", None, None),
        P("level", "sub", None, None),
        P("sub", "rhs", None),
        P(),
    )
    return jax.shard_map(
        body,
        mesh=mesh,
        in_specs=placed,
        out_specs=(P("level", "sub", "rhs", None), P("level", "sub", "rhs", None)),
        check_vma=False,
    )
```

```python
import functools

import jax
import jax.numpy as jnp
from jax import lax
from jax.experimental import pallas as pl
from jax.experimental.pallas import tpu as pltpu
from jax.sharding import PartitionSpec as P

MESH = pl.DeviceIdType.MESH
CHUNK = 8
LAG = 4


def other(sub, mask):
    return sub + mask - 2 * mask * ((sub // mask) % 2)


def kernel(
    parent, rhs_in, linv_in, loff_in, uinv_in, uoff_in, anc_in,
    sol_out, upd_out,
    rhs, linv, loff, uinv, uoff, anc, sol, upd,
    sel, res, fwd, snd, inc, crecv, hbuf, back, above, stage,
    in_sem, piece_sem, out_sem, fs, fr, bs, br, cs, cr,
):
    count, rows, width = rhs.shape
    size = CHUNK
    chunks = rows // size
    level = lax.axis_index("level")
    sub = lax.axis_index("sub")
    col = lax.axis_index("rhs")
    top = 3

    def at(lv, s):
        return (lv, s, col)

    def cut(k):
        return pl.ds(pl.multiple_of(k * size, size), size)

    loads = [
        pltpu.make_async_copy(uoff_in, uoff, in_sem.at[3]),
        pltpu.make_async_copy(uinv_in, uinv, in_sem.at[4]),
    ]
    first = pltpu.make_async_copy(
        rhs_in.at[:, cut(0), :], rhs.at[:, cut(0), :], in_sem.at[0]
    )
    later = pl.ds(size, rows - size)
    rest = pltpu.make_async_copy(
        rhs_in.at[:, later, :], rhs.at[:, later, :], in_sem.at[1]
    )
    quarter = count // 4
    pieces = []
    for i, (source, target) in enumerate(((linv_in, linv), (loff_in, loff))):
        for j in range(4):
            where = pl.ds(j * quarter, quarter)
            pieces.append(
                pltpu.make_async_copy(
                    source.at[where], target.at[where], piece_sem.at[i, j]
                )
            )
    first.start()
    for piece in pieces:
        piece.start()
    rest.start()

    def anc_load(k):
        return pltpu.make_async_copy(
            anc_in.at[:, cut(k), :], anc.at[k], in_sem.at[5 + k]
        )

    barrier = pltpu.get_barrier_semaphore()
    friends = {
        0: [(0, 1), (1, 0)],
        1: [(0, 0), (1, 2), (2, 0), (2, 2)],
        2: [(1, 0), (1, 2), (2, 4), (3, 0), (3, 4)],
        3: [(2, 0), (2, 4)],
    }
    for lv, group in friends.items():
        @pl.when(level == lv)
        def _():
            for to, mask in group:
                there = other(sub, mask) if mask else sub
                pl.semaphore_signal(
                    barrier, inc=1, device_id=at(to, there), device_id_type=MESH
                )

    row = jnp.minimum(level, top - 1)
    codes = []
    for c in range(count):
        p = parent[row, sub * count + c]
        codes.append((p % count) + jnp.where(p // count == sub, 0, count))
    lane = lax.broadcasted_iota(jnp.int32, (1, count * size), 1)
    target = jnp.zeros((1, count * size), jnp.int32)
    for c in range(count):
        target = jnp.where(lane // size == c, codes[c], target)
    target = target * size + lane % size
    down = lax.broadcasted_iota(jnp.int32, (2 * count * size, count * size), 0)
    sel[...] = (down == target).astype(jnp.bfloat16)

    for lv, group in friends.items():
        @pl.when(level == lv)
        def _():
            pl.semaphore_wait(barrier, len(group))

    def remote(src, dst, ss, rs, to):
        return pltpu.make_async_remote_copy(
            src_ref=src, dst_ref=dst, send_sem=ss, recv_sem=rs,
            device_id=to, device_id_type=MESH,
        )

    def up_home(k, lv):
        return remote(
            snd.at[k, 0], inc.at[k], fs.at[k], fr.at[k], at(lv + 1, sub),
        )

    def down_home(k, lv):
        return remote(
            back.at[k], above.at[k, pl.ds(0, count)],
            bs.at[k, 0], br.at[k, 0], at(lv - 1, sub),
        )

    def down_far(k, lv):
        return remote(
            back.at[k], above.at[k, pl.ds(count, count)],
            bs.at[k, 1], br.at[k, 1], at(lv - 1, other(sub, 2 ** (lv - 1))),
        )

    def side_up(k, lv):
        return remote(
            snd.at[k, 1], crecv.at[k],
            cs.at[k, 0], cr.at[k, 0], at(lv, other(sub, 2**lv)),
        )

    def side_down(k):
        return remote(
            above.at[k, pl.ds(0, count)], above.at[k, pl.ds(count, count)],
            cs.at[k, 1], cr.at[k, 1], at(0, other(sub, 1)),
        )

    def upd_store(k):
        return pltpu.make_async_copy(
            upd.at[:, cut(k), :], upd_out.at[:, cut(k), :], out_sem.at[k, 0]
        )

    def sol_store(k):
        return pltpu.make_async_copy(
            sol.at[:, cut(k), :], sol_out.at[:, cut(k), :], out_sem.at[k, 1]
        )

    def forward(k):
        @pl.when(k == 0)
        def _():
            first.wait()

        @pl.when(k == 1)
        def _():
            rest.wait()

        @pl.when(level == 0)
        def _():
            res[...] = rhs[:, cut(k), :].astype(jnp.bfloat16)

        @pl.when(level > 0)
        def _():
            up_home(k, 0).wait_recv()
            got = inc[k].astype(jnp.float32)
            res[...] = (rhs[:, cut(k), :] - got).astype(jnp.bfloat16)

        @pl.when(k == 0)
        def _():
            for piece in pieces[:4]:
                piece.wait()

        for c in range(count):
            part = jnp.dot(res[c], linv[c], preferred_element_type=jnp.float32)
            fwd[k, c] = part.astype(jnp.bfloat16)

        @pl.when(k == 0)
        def _():
            for piece in pieces[4:]:
                piece.wait()
            for load in loads:
                load.start()

        @pl.when((k == 0) & (level == top))
        def _():
            for j in range(chunks):
                anc_load(j).start()

        for c in range(count):
            upd[c, cut(k), :] = jnp.dot(
                fwd[k, c], loff[c], preferred_element_type=jnp.float32
            )
        upd_store(k).start()

        @pl.when(level < top)
        def _():
            moved = upd[:, cut(k), :].reshape(count * size, width)
            moved = moved.astype(jnp.bfloat16)

            def sums(half):
                rows_of = sel[pl.ds(half * count * size, count * size)]
                total = jnp.dot(rows_of, moved, preferred_element_type=jnp.float32)
                return total.reshape(count, size, width)

            snd[k, 1] = sums(1).astype(jnp.bfloat16)
            for lv in (0, 1, 2):
                @pl.when(level == lv)
                def _():
                    side_up(k, lv).start()
            hbuf[k] = sums(0)

    def settle(k, lv):
        side_up(k, lv).wait_recv()
        total = hbuf[k] + crecv[k].astype(jnp.float32)
        snd[k, 0] = total.astype(jnp.bfloat16)
        up_home(k, lv).start()

    def relay(k):
        down_home(k, 1).wait_recv()
        side_down(k).start()

    def backward(k):
        @pl.when(k == 0)
        def _():
            for load in loads:
                load.wait()

        @pl.when(level == top)
        def _():
            anc_load(k).wait()
            stage[pl.ds(0, count)] = anc[k]

        @pl.when((level == 1) | (level == 2))
        def _():
            down_home(k, 2).wait_recv()
            down_far(k, 2).wait_recv()
            stage[...] = above[k]

        @pl.when(level == 0)
        def _():
            side_down(k).wait_recv()
            stage[...] = above[k]

        for c in range(count):
            where = jnp.where(level == top, c, codes[c])
            term = jnp.dot(stage[where], uoff[c], preferred_element_type=jnp.float32)
            res[c] = (fwd[k, c].astype(jnp.float32) - term).astype(jnp.bfloat16)
        for c in range(count):
            part = jnp.dot(res[c], uinv[c], preferred_element_type=jnp.float32)
            sol[c, cut(k), :] = part
            back[k, c] = part.astype(jnp.bfloat16)
        for lv in (1, 2, 3):
            @pl.when(level == lv)
            def _():
                down_home(k, lv).start()
                if lv > 1:
                    down_far(k, lv).start()
        sol_store(k).start()

    lag = jnp.where(level == top, -1, jnp.where(level == 2, min(LAG, chunks), chunks))

    def step(i, carry):
        @pl.when(i < chunks)
        def _():
            forward(i)

        for lv in (0, 1, 2):
            @pl.when((level == lv) & (i >= 1) & (i <= chunks))
            def _():
                settle(i - 1, lv)

        @pl.when((level == 0) & (i >= lag) & (i < chunks + lag))
        def _():
            relay(i - lag)

        @pl.when(i > lag)
        def _():
            backward(i - lag - 1)

        return carry

    lax.fori_loop(0, chunks + lag + 1, step, 0)

    def finish(k, carry):
        upd_store(k).wait()
        sol_store(k).wait()

        for lv in (0, 1, 2):
            @pl.when(level == lv)
            def _():
                up_home(k, lv).wait_send()
                side_up(k, lv).wait_send()
                if lv == 0:
                    side_down(k).wait_send()

        for lv in (1, 2, 3):
            @pl.when(level == lv)
            def _():
                down_home(k, lv).wait_send()
                if lv > 1:
                    down_far(k, lv).wait_send()

        return carry

    lax.fori_loop(0, chunks, finish, 0)


def body(rhs, lower_inv, lower_off, upper_inv, upper_off, ancestor, parent):
    count, rows, width = rhs.shape[1:]
    size = CHUNK
    chunks = rows // size
    f32, b16 = jnp.float32, jnp.bfloat16
    vm = pltpu.VMEM
    sem = pltpu.SemaphoreType.DMA
    anyspace = pl.BlockSpec(memory_space=pl.ANY)
    sol, upd = pl.pallas_call(
        kernel,
        out_shape=(vm((count, rows, width), f32), vm((count, rows, width), f32)),
        in_specs=[pl.BlockSpec(memory_space=pltpu.SMEM)] + [anyspace] * 6,
        out_specs=(anyspace, anyspace),
        scratch_shapes=[
            vm((count, rows, width), f32),
            vm((count, width, width), b16),
            vm((count, width, width), b16),
            vm((count, width, width), b16),
            vm((count, width, width), b16),
            vm((chunks, count, size, width), b16),
            vm((count, rows, width), f32),
            vm((count, rows, width), f32),
            vm((2 * count * size, count * size), b16),
            vm((count, size, width), b16),
            vm((chunks, count, size, width), b16),
            vm((chunks, 2, count, size, width), b16),
            vm((chunks, count, size, width), b16),
            vm((chunks, count, size, width), b16),
            vm((chunks, count, size, width), f32),
            vm((chunks, count, size, width), b16),
            vm((chunks, 2 * count, size, width), b16),
            vm((2 * count, size, width), b16),
            sem((5 + chunks,)),
            sem((2, 4)),
            sem((chunks, 2)),
            sem((chunks,)),
            sem((chunks,)),
            sem((chunks, 2)),
            sem((chunks, 2)),
            sem((chunks, 2)),
            sem((chunks, 2)),
        ],
        compiler_params=pltpu.CompilerParams(
            collective_id=0, has_side_effects=True, vmem_limit_bytes=58 * 2**20
        ),
        name="tree_solve",
    )(parent, rhs[0], lower_inv[0], lower_off[0], upper_inv[0], upper_off[0], ancestor)
    return (sol[None], upd[None])


def solution(mesh):
    placed = (
        P("level", "sub", "rhs", None),
        P("level", "sub", None, None),
        P("level", "sub", None, None),
        P("level", "sub", None, None),
        P("level", "sub", None, None),
        P("sub", "rhs", None),
        P(),
    )
    return jax.shard_map(
        body,
        mesh=mesh,
        in_specs=placed,
        out_specs=(P("level", "sub", "rhs", None), P("level", "sub", "rhs", None)),
        check_vma=False,
    )
```

```python
import functools

import jax
import jax.numpy as jnp
from jax import lax
from jax.experimental import pallas as pl
from jax.experimental.pallas import tpu as pltpu
from jax.sharding import PartitionSpec as P

MESH = pl.DeviceIdType.MESH
CHUNK = 8
LAG = 4


def other(sub, mask):
    return sub + mask - 2 * mask * ((sub // mask) % 2)


def kernel(
    parent, rhs_in, linv_in, loff_in, uinv_in, uoff_in, anc_in,
    sol_out, upd_out,
    rhs, linv, loff, uinv, uoff, anc, sol, upd,
    sel, res, fwd, snd, inc, crecv, hbuf, back, above, stage,
    in_sem, piece_sem, out_sem, fs, fr, bs, br, cs, cr,
):
    count, rows, width = rhs.shape
    size = CHUNK
    chunks = rows // size
    level = lax.axis_index("level")
    sub = lax.axis_index("sub")
    col = lax.axis_index("rhs")
    top = 3

    def at(lv, s):
        return (lv, s, col)

    def cut(k):
        return pl.ds(pl.multiple_of(k * size, size), size)

    loads = [
        pltpu.make_async_copy(uoff_in, uoff, in_sem.at[3]),
        pltpu.make_async_copy(uinv_in, uinv, in_sem.at[4]),
    ]
    first = pltpu.make_async_copy(
        rhs_in.at[:, cut(0), :], rhs.at[:, cut(0), :], in_sem.at[0]
    )
    later = pl.ds(size, rows - size)
    rest = pltpu.make_async_copy(
        rhs_in.at[:, later, :], rhs.at[:, later, :], in_sem.at[1]
    )
    quarter = count // 4
    pieces = []
    for i, (source, target) in enumerate(((linv_in, linv), (loff_in, loff))):
        for j in range(4):
            where = pl.ds(j * quarter, quarter)
            pieces.append(
                pltpu.make_async_copy(
                    source.at[where], target.at[where], piece_sem.at[i, j]
                )
            )
    first.start()
    for piece in pieces:
        piece.start()
    rest.start()

    def anc_load(k):
        return pltpu.make_async_copy(
            anc_in.at[:, cut(k), :], anc.at[k], in_sem.at[5 + k]
        )

    barrier = pltpu.get_barrier_semaphore()
    friends = {
        0: [(0, 1), (1, 0)],
        1: [(0, 0), (1, 2), (2, 0), (2, 2)],
        2: [(1, 0), (1, 2), (2, 4), (3, 0), (3, 4)],
        3: [(2, 0), (2, 4)],
    }
    for lv, group in friends.items():
        @pl.when(level == lv)
        def _():
            for to, mask in group:
                there = other(sub, mask) if mask else sub
                pl.semaphore_signal(
                    barrier, inc=1, device_id=at(to, there), device_id_type=MESH
                )

    row = jnp.minimum(level, top - 1)
    codes = []
    for c in range(count):
        p = parent[row, sub * count + c]
        codes.append((p % count) + jnp.where(p // count == sub, 0, count))
    lane = lax.broadcasted_iota(jnp.int32, (1, count * size), 1)
    target = jnp.zeros((1, count * size), jnp.int32)
    for c in range(count):
        target = jnp.where(lane // size == c, codes[c], target)
    target = target * size + lane % size
    down = lax.broadcasted_iota(jnp.int32, (2 * count * size, count * size), 0)
    sel[...] = (down == target).astype(jnp.bfloat16)

    def remote(src, dst, ss, rs, to):
        return pltpu.make_async_remote_copy(
            src_ref=src, dst_ref=dst, send_sem=ss, recv_sem=rs,
            device_id=to, device_id_type=MESH,
        )

    def up_home(k, lv):
        return remote(
            snd.at[k, 0], inc.at[k], fs.at[k], fr.at[k], at(lv + 1, sub),
        )

    def down_home(k, lv):
        return remote(
            back.at[k], above.at[k, pl.ds(0, count)],
            bs.at[k, 0], br.at[k, 0], at(lv - 1, sub),
        )

    def down_far(k, lv):
        return remote(
            back.at[k], above.at[k, pl.ds(count, count)],
            bs.at[k, 1], br.at[k, 1], at(lv - 1, other(sub, 2 ** (lv - 1))),
        )

    def side_up(k, lv):
        return remote(
            snd.at[k, 1], crecv.at[k],
            cs.at[k, 0], cr.at[k, 0], at(lv, other(sub, 2**lv)),
        )

    def side_down(k):
        return remote(
            above.at[k, pl.ds(0, count)], above.at[k, pl.ds(count, count)],
            cs.at[k, 1], cr.at[k, 1], at(0, other(sub, 1)),
        )

    def upd_store(k):
        return pltpu.make_async_copy(
            upd.at[:, cut(k), :], upd_out.at[:, cut(k), :], out_sem.at[k, 0]
        )

    def sol_store(k):
        return pltpu.make_async_copy(
            sol.at[:, cut(k), :], sol_out.at[:, cut(k), :], out_sem.at[k, 1]
        )

    def forward(k):
        @pl.when(k == 0)
        def _():
            first.wait()

        @pl.when(k == 1)
        def _():
            rest.wait()

        @pl.when(level == 0)
        def _():
            res[...] = rhs[:, cut(k), :].astype(jnp.bfloat16)

        @pl.when(level > 0)
        def _():
            up_home(k, 0).wait_recv()
            got = inc[k].astype(jnp.float32)
            res[...] = (rhs[:, cut(k), :] - got).astype(jnp.bfloat16)

        @pl.when(k == 0)
        def _():
            for piece in pieces[:4]:
                piece.wait()

        for c in range(count):
            part = jnp.dot(res[c], linv[c], preferred_element_type=jnp.float32)
            fwd[k, c] = part.astype(jnp.bfloat16)

        @pl.when(k == 0)
        def _():
            for piece in pieces[4:]:
                piece.wait()
            for load in loads:
                load.start()

        @pl.when((k == 0) & (level == top))
        def _():
            for j in range(chunks):
                anc_load(j).start()

        for c in range(count):
            upd[c, cut(k), :] = jnp.dot(
                fwd[k, c], loff[c], preferred_element_type=jnp.float32
            )
        upd_store(k).start()

        for lv, group in friends.items():
            @pl.when((k == 0) & (level == lv))
            def _():
                pl.semaphore_wait(barrier, len(group))

        @pl.when(level < top)
        def _():
            moved = upd[:, cut(k), :].reshape(count * size, width)
            moved = moved.astype(jnp.bfloat16)

            def sums(half):
                rows_of = sel[pl.ds(half * count * size, count * size)]
                total = jnp.dot(rows_of, moved, preferred_element_type=jnp.float32)
                return total.reshape(count, size, width)

            snd[k, 1] = sums(1).astype(jnp.bfloat16)
            for lv in (0, 1, 2):
                @pl.when(level == lv)
                def _():
                    side_up(k, lv).start()
            hbuf[k] = sums(0)

    def settle(k, lv):
        side_up(k, lv).wait_recv()
        total = hbuf[k] + crecv[k].astype(jnp.float32)
        snd[k, 0] = total.astype(jnp.bfloat16)
        up_home(k, lv).start()

    def relay(k):
        down_home(k, 1).wait_recv()
        side_down(k).start()

    def backward(k):
        @pl.when(k == 0)
        def _():
            for load in loads:
                load.wait()

        @pl.when(level == top)
        def _():
            anc_load(k).wait()
            stage[pl.ds(0, count)] = anc[k]

        @pl.when((level == 1) | (level == 2))
        def _():
            down_home(k, 2).wait_recv()
            down_far(k, 2).wait_recv()
            stage[...] = above[k]

        @pl.when(level == 0)
        def _():
            side_down(k).wait_recv()
            stage[...] = above[k]

        for c in range(count):
            where = jnp.where(level == top, c, codes[c])
            term = jnp.dot(stage[where], uoff[c], preferred_element_type=jnp.float32)
            res[c] = (fwd[k, c].astype(jnp.float32) - term).astype(jnp.bfloat16)
        for c in range(count):
            part = jnp.dot(res[c], uinv[c], preferred_element_type=jnp.float32)
            sol[c, cut(k), :] = part
            back[k, c] = part.astype(jnp.bfloat16)
        for lv in (1, 2, 3):
            @pl.when(level == lv)
            def _():
                if lv > 1:
                    down_far(k, lv).start()
                down_home(k, lv).start()
        sol_store(k).start()

    lag = jnp.where(level == top, -1, jnp.where(level == 2, min(LAG, chunks), chunks))

    def step(i, carry):
        @pl.when(i < chunks)
        def _():
            forward(i)

        for lv in (0, 1, 2):
            @pl.when((level == lv) & (i >= 1) & (i <= chunks))
            def _():
                settle(i - 1, lv)

        @pl.when((level == 0) & (i >= lag) & (i < chunks + lag))
        def _():
            relay(i - lag)

        @pl.when(i > lag)
        def _():
            backward(i - lag - 1)

        return carry

    lax.fori_loop(0, chunks + lag + 1, step, 0)

    def finish(k, carry):
        upd_store(k).wait()
        sol_store(k).wait()

        for lv in (0, 1, 2):
            @pl.when(level == lv)
            def _():
                up_home(k, lv).wait_send()
                side_up(k, lv).wait_send()
                if lv == 0:
                    side_down(k).wait_send()

        for lv in (1, 2, 3):
            @pl.when(level == lv)
            def _():
                down_home(k, lv).wait_send()
                if lv > 1:
                    down_far(k, lv).wait_send()

        return carry

    lax.fori_loop(0, chunks, finish, 0)


def body(rhs, lower_inv, lower_off, upper_inv, upper_off, ancestor, parent):
    count, rows, width = rhs.shape[1:]
    size = CHUNK
    chunks = rows // size
    f32, b16 = jnp.float32, jnp.bfloat16
    vm = pltpu.VMEM
    sem = pltpu.SemaphoreType.DMA
    anyspace = pl.BlockSpec(memory_space=pl.ANY)
    sol, upd = pl.pallas_call(
        kernel,
        out_shape=(vm((count, rows, width), f32), vm((count, rows, width), f32)),
        in_specs=[pl.BlockSpec(memory_space=pltpu.SMEM)] + [anyspace] * 6,
        out_specs=(anyspace, anyspace),
        scratch_shapes=[
            vm((count, rows, width), f32),
            vm((count, width, width), b16),
            vm((count, width, width), b16),
            vm((count, width, width), b16),
            vm((count, width, width), b16),
            vm((chunks, count, size, width), b16),
            vm((count, rows, width), f32),
            vm((count, rows, width), f32),
            vm((2 * count * size, count * size), b16),
            vm((count, size, width), b16),
            vm((chunks, count, size, width), b16),
            vm((chunks, 2, count, size, width), b16),
            vm((chunks, count, size, width), b16),
            vm((chunks, count, size, width), b16),
            vm((chunks, count, size, width), f32),
            vm((chunks, count, size, width), b16),
            vm((chunks, 2 * count, size, width), b16),
            vm((2 * count, size, width), b16),
            sem((5 + chunks,)),
            sem((2, 4)),
            sem((chunks, 2)),
            sem((chunks,)),
            sem((chunks,)),
            sem((chunks, 2)),
            sem((chunks, 2)),
            sem((chunks, 2)),
            sem((chunks, 2)),
        ],
        compiler_params=pltpu.CompilerParams(
            collective_id=0, has_side_effects=True, vmem_limit_bytes=58 * 2**20
        ),
        name="tree_solve",
    )(parent, rhs[0], lower_inv[0], lower_off[0], upper_inv[0], upper_off[0], ancestor)
    return (sol[None], upd[None])


def solution(mesh):
    placed = (
        P("level", "sub", "rhs", None),
        P("level", "sub", None, None),
        P("level", "sub", None, None),
        P("level", "sub", None, None),
        P("level", "sub", None, None),
        P("sub", "rhs", None),
        P(),
    )
    return jax.shard_map(
        body,
        mesh=mesh,
        in_specs=placed,
        out_specs=(P("level", "sub", "rhs", None), P("level", "sub", "rhs", None)),
        check_vma=False,
    )
```
